32 devices in a mesh: row: 4 (over y, x), col: 8 (over z, core).
Axes of the slice: x: 2, y: 2, z: 4, core: 2. Of those that a mesh axis runs over, the one named last changes fastest.
Arguments:
- known_inverse: float32 [12288, 12288], P('col', 'row'), may hold values from -6 to 6
- factor_sep: float32 [12288, 1536], P('col'), may hold values from -0.09375 to 0.09375
- factor_pair: float32 [1536, 1536], P('col'), may hold values from -0.25 to 0.25
- pivot_inverse: float32 [1536, 1536], P('col', 'row'), may hold values from -6 to 6
- widths: int32 [8], replicated, may hold values from 1 to 512, 1536 in all
- parent_of: int32 [8], replicated, may hold values from -1 to 7, as said below
- ancestors: int32 [8, 24], replicated, may hold values from 0 to 63, all different within a row
Outputs:
- panel_inverse: float32 [1536, 12288], P('col', 'row')
- block_inverse: float32 [1536, 1536], P('col', 'row')
The draws below stay inside these ranges and needn't reach their ends.
Inputs may be any that keep to these rules, and one draw needn't show every extreme that they name: `parent_of`: exactly 4 supernodes have -1; each other one names one of those. `ancestors`: each supernode lists different blocks; every block is listed by some supernode. The widths sum to 1536.
All inputs are finite; a program needn't handle non-finite values.
Results may differ from the reference program's by a relative error of at most 0.0003.
Values sent between devices are 32-bit elements; how exact they have to be, the bound alone decides.
A program may use at most 192 MiB of HBM per device.

```python
import math
import jax
import jax.numpy as jnp
import numpy as np
from jax import lax

NS = 12288
WTOT = 1536
NSUP = 8
NUP = 4
NBLK = 64
ANC = 24
WMOST = 512


def draw_parent_of(key, part):
    order_key, pick_key = jax.random.split(jax.random.fold_in(key, 11))
    ordering = jax.random.permutation(order_key, NSUP).astype(jnp.int32)
    position = jnp.argsort(ordering).astype(jnp.int32)
    is_upper = position < NUP
    chosen = jax.random.randint(pick_key, (NSUP,), 0, NUP).astype(jnp.int32)
    parents = ordering[chosen]
    return jnp.where(is_upper, -1, parents).astype(jnp.int32)


def steps_of(own_key, extent, cuts, least, top_value):
    def one(dim, parts):
        draws = jax.random.uniform(jax.random.fold_in(jax.random.fold_in(own_key, 6), dim), (parts,), jnp.float32, least / len(cuts), top_value / len(cuts))
        return jnp.repeat(jnp.exp(draws), extent[dim] // parts).reshape((-1,) + (1,) * (len(extent) - dim - 1))

    gain = one(*cuts[0])
    for cut in cuts[1:]:
        gain = gain * one(*cut)
    return gain


def choose_distinct(key, rows, number_of, top, lift):
    ranking = jax.random.permutation(jax.random.fold_in(key, 1), number_of)
    boost = ranking
    for power in range(3):
        boost = boost * boost // number_of
    boost = boost * lift // number_of
    tickets = jax.random.randint(jax.random.fold_in(key, 2), (rows, number_of), 0, 4096) + boost
    holders = jax.random.permutation(jax.random.fold_in(key, 3), rows)[jnp.arange(number_of) % rows]
    tickets = jnp.where(jnp.arange(rows)[:, None] == holders[None, :], 1 << 14, tickets)
    score = tickets * number_of + jnp.arange(number_of)
    return lax.top_k(score.astype(jnp.int32), top)[1].astype(jnp.int32)


def split_up(amount, total, reach, lean):
    loads = [(1 << 20) // math.isqrt(standing ** lean) + 1 for standing in range(2, amount + 1)]
    surplus, holding = total - reach - (amount - 1), [1] * (amount - 1)
    while surplus > 0:
        free = [i for i in range(amount - 1) if holding[i] < reach]
        whole, budget = sum([loads[i] for i in free]), surplus
        for i in free:
            extra = min(reach - holding[i], max(1, budget * loads[i] // whole), surplus)
            holding[i] = holding[i] + extra
            surplus = surplus - extra
    return np.array([reach] + holding)


def uneven_parts(own_key, count, total, most, skew):
    if count == 2:
        one = jax.random.randint(own_key, (), max(1, total - most), min(most, total - 1) + 1)
        return jnp.stack([one, total - one])
    tallies = jnp.asarray(split_up(count, total, most, skew), jnp.int32)
    couples = (count - 1) // 2
    source_of, receiver = tallies[1:1 + 2 * couples:2], tallies[2:2 + 2 * couples:2]
    slack = jnp.minimum(source_of - 1, most - receiver)
    moved = jax.random.randint(jax.random.fold_in(own_key, 1), (couples,), 0, 1 << 20) % (slack + 1)
    tallies = tallies.at[1:1 + 2 * couples:2].set(source_of - moved).at[2:2 + 2 * couples:2].set(receiver + moved)
    return tallies[jax.random.permutation(jax.random.fold_in(own_key, 2), count)]


def centred(key, shape, spread, bound, pieces=(), held_as=jnp.bfloat16):
    entries = spread * jax.random.normal(key, shape, jnp.float32)
    if pieces:
        entries = entries * steps_of(key, shape, pieces, -0.22, 0.18)
    return jnp.clip(entries, -bound, bound).astype(held_as)


def setup_inputs(seed: int = 0) -> dict:
    arg_keys = jax.random.split(jax.random.key(seed), 8)
    known_inverse = centred(arg_keys[0], (NS, NS), 1.0, 6.0, ((0, 8), (1, 4)), jnp.float32)
    factor_sep = centred(arg_keys[1], (NS, WTOT), (NS * ANC // NBLK) ** -0.5, 0.09375, ((0, 8),), jnp.float32)
    factor_pair = centred(arg_keys[2], (WTOT, WTOT), WMOST ** -0.5, 0.25, ((0, 8),), jnp.float32)
    pivot_inverse = centred(arg_keys[3], (WTOT, WTOT), 1.0, 6.0, ((0, 8), (1, 4)), jnp.float32)
    widths = uneven_parts(arg_keys[4], NSUP, WTOT, WMOST, 2).astype(jnp.int32)
    parent_of = draw_parent_of(jax.random.fold_in(arg_keys[7], 71), 0)
    ancestors = choose_distinct(arg_keys[6], NSUP, NBLK, ANC, 6144)
    return {"known_inverse": known_inverse, "factor_sep": factor_sep, "factor_pair": factor_pair, "pivot_inverse": pivot_inverse, "widths": widths, "parent_of": parent_of, "ancestors": ancestors}


exact_mode = lax.Precision.HIGHEST


def plain_dot(left, right):
    return jnp.dot(left, right, precision=exact_mode, preferred_element_type=jnp.float32)


def first_dot(left, right):
    return lax.dot_general(left, right, (((0,), (0,)), ((), ())), precision=exact_mode, preferred_element_type=jnp.float32)


def supernode_tables(widths, parent_of, ancestors):
    position = jnp.arange(WTOT, dtype=jnp.int32)
    width_ends = jnp.cumsum(widths).astype(jnp.int32)
    column_owner = jnp.sum((width_ends[None, :] <= position[:, None]).astype(jnp.int32), axis=1).astype(jnp.int32)
    owner_onehot = column_owner[:, None] == jnp.arange(NSUP, dtype=jnp.int32)[None, :]
    listed = jnp.any(ancestors[:, :, None] == jnp.arange(NBLK, dtype=jnp.int32)[None, None, :], axis=1).astype(jnp.float32)
    column_blocks = plain_dot(owner_onehot.astype(jnp.float32), listed)
    column_parent = jnp.sum(jnp.where(owner_onehot, parent_of[None, :], 0), axis=1).astype(jnp.int32)
    column_upper = column_parent < 0
    return column_owner, column_blocks, column_parent, column_upper


def reference(known_inverse, factor_sep, factor_pair, pivot_inverse, widths, parent_of, ancestors):
    column_owner, column_blocks, column_parent, column_upper = supernode_tables(widths, parent_of, ancestors)
    sep_index = jnp.arange(NS, dtype=jnp.int32)
    block_onehot = ((sep_index // (NS // NBLK))[:, None] == jnp.arange(NBLK, dtype=jnp.int32)[None, :]).astype(jnp.float32)
    sep_factor = factor_sep * plain_dot(block_onehot, column_blocks.T)
    upper_cols = column_upper.astype(jnp.float32)
    lower_cols = 1.0 - upper_cols
    coupling = jnp.where((column_owner[:, None] == column_parent[None, :]) & (~column_upper)[None, :], factor_pair, 0.0)
    matching = column_owner[:, None] == column_owner[None, :]
    upper_factor = sep_factor * upper_cols[None, :]
    lower_factor = sep_factor * lower_cols[None, :]
    product = -first_dot(sep_factor, known_inverse)
    panel_upper = product * upper_cols[:, None]
    upper_block = jnp.where(matching & column_upper[None, :], pivot_inverse - plain_dot(panel_upper, upper_factor), 0.0)
    panel_lower = product * lower_cols[:, None] - first_dot(coupling, panel_upper)
    pair_block = jnp.where(column_owner[:, None] == column_parent[None, :], -(plain_dot(panel_upper, lower_factor) + plain_dot(upper_block, coupling)), 0.0)
    lower_block = jnp.where(matching & (~column_upper)[None, :], pivot_inverse - plain_dot(panel_lower, lower_factor) - first_dot(pair_block, coupling), 0.0)
    return panel_upper + panel_lower, upper_block + lower_block + pair_block
```

```python
import jax
import jax.numpy as jnp
from jax import lax
from jax.sharding import PartitionSpec as P

NS = 12288
WTOT = 1536
NSUP = 8
NBLK = 64


exact_mode = lax.Precision.HIGH
panel_chunks = 4


def plain_dot(left, right):
    return jnp.dot(left, right, precision=exact_mode, preferred_element_type=jnp.float32)


def first_dot(left, right):
    return lax.dot_general(
        left,
        right,
        (((0,), (0,)), ((), ())),
        precision=exact_mode,
        preferred_element_type=jnp.float32,
    )


def supernode_tables(widths, parent_of, ancestors):
    position = jnp.arange(WTOT, dtype=jnp.int32)
    width_ends = jnp.cumsum(widths)
    column_owner = jnp.sum((width_ends[None, :] <= position[:, None]).astype(jnp.int32), axis=1)
    owner_onehot = column_owner[:, None] == jnp.arange(NSUP, dtype=jnp.int32)[None, :]
    listed = jnp.any(
        ancestors[:, :, None] == jnp.arange(NBLK, dtype=jnp.int32)[None, None, :], axis=1
    ).astype(jnp.float32)
    column_blocks = plain_dot(owner_onehot.astype(jnp.float32), listed)
    column_parent = jnp.sum(jnp.where(owner_onehot, parent_of[None, :], 0), axis=1)
    column_upper = column_parent < 0
    return (column_owner, column_blocks, column_parent, column_upper)


def shards(known_inverse, factor_sep, factor_pair, pivot_inverse, widths, parent_of, ancestors):
    col_index = lax.axis_index("col")
    row_index = lax.axis_index("row")
    rows = lax.axis_size("row")
    cols = lax.axis_size("col")
    fold_ratio = cols // rows
    sep_local = factor_sep.shape[0]
    pair_local = factor_pair.shape[0]
    wide_local = pivot_inverse.shape[1]
    column_owner, column_blocks, column_parent, column_upper = supernode_tables(
        widths, parent_of, ancestors
    )
    sep_index = col_index * sep_local + jnp.arange(sep_local, dtype=jnp.int32)
    block_onehot = (
        (sep_index // (NS // NBLK))[:, None] == jnp.arange(NBLK, dtype=jnp.int32)[None, :]
    ).astype(jnp.float32)
    sep_factor = factor_sep * plain_dot(block_onehot, column_blocks.T)
    upper_cols = column_upper.astype(jnp.float32)
    lower_cols = 1.0 - upper_cols
    owner_rows = lax.dynamic_slice_in_dim(column_owner, col_index * pair_local, pair_local)
    owner_wide = lax.dynamic_slice_in_dim(column_owner, row_index * wide_local, wide_local)
    parent_wide = lax.dynamic_slice_in_dim(column_parent, row_index * wide_local, wide_local)
    upper_rows = lax.dynamic_slice_in_dim(upper_cols, col_index * pair_local, pair_local)
    upper_wide = lax.dynamic_slice_in_dim(column_upper, row_index * wide_local, wide_local)
    coupling = jnp.where(
        (owner_rows[:, None] == column_parent[None, :]) & (~column_upper)[None, :], factor_pair, 0.0
    )
    matching = owner_rows[:, None] == owner_wide[None, :]
    match_lower = matching & (~upper_wide)[None, :]
    match_pair = owner_rows[:, None] == parent_wide[None, :]
    match_upper_all = (owner_rows[:, None] == column_owner[None, :]) & column_upper[None, :]

    coupling_all = lax.all_gather(coupling, "col", axis=0, tiled=True)

    piece_rows = sep_local // rows
    piece = lax.dynamic_slice_in_dim(sep_factor, row_index * piece_rows, piece_rows)
    deal = [
        (r * cols + c, (c // fold_ratio) * cols + (c % fold_ratio) * rows + r)
        for r in range(rows)
        for c in range(cols)
    ]
    piece = lax.ppermute(piece, ("row", "col"), deal)
    piece, coupling_all = lax.optimization_barrier((piece, coupling_all))
    sep_cols = lax.all_gather(piece, "col", axis=0, tiled=True)

    lead = plain_dot(sep_factor * upper_cols[None, :], coupling_all) - sep_factor
    step = known_inverse.shape[1] // panel_chunks
    panels = []
    product = jnp.zeros((pair_local, WTOT), jnp.float32)
    for i in range(panel_chunks):
        part = first_dot(lead, known_inverse[:, i * step : (i + 1) * step])
        panels.append(lax.psum_scatter(part, "col", scatter_dimension=0, tiled=True))
    for i in range(panel_chunks):
        product = product + plain_dot(panels[i], sep_cols[i * step : (i + 1) * step])
    panel = jnp.concatenate(panels, 1)

    own_pivot = lax.dynamic_update_slice_in_dim(
        jnp.zeros_like(product), jnp.where(matching, pivot_inverse, 0.0), row_index * wide_local, 1
    )
    deficit = lax.psum(product - own_pivot, "row")
    upper_block_all = jnp.where(match_upper_all, -deficit, 0.0)
    pair_rows = -(
        deficit * upper_rows[:, None] * lower_cols[None, :]
        + plain_dot(upper_block_all, coupling_all)
    )
    pair_cols = lax.all_to_all(pair_rows, "col", split_axis=1, concat_axis=0, tiled=True)
    coupling_own = lax.dynamic_slice_in_dim(coupling_all, row_index * wide_local, wide_local, 1)

    def own_cols(x):
        return lax.dynamic_slice_in_dim(x, row_index * wide_local, wide_local, 1)

    pair_block = jnp.where(match_pair, own_cols(pair_rows), 0.0)
    lower_block = jnp.where(
        match_lower, -own_cols(deficit) - first_dot(pair_cols, coupling_own), 0.0
    )
    return (panel, own_cols(upper_block_all) + lower_block + pair_block)


def solution(mesh):
    in_specs = (P("col", "row"), P("col", None), P("col", None), P("col", "row"), P(), P(), P())
    out_specs = (P("col", "row"), P("col", "row"))
    return jax.shard_map(shards, mesh=mesh, in_specs=in_specs, out_specs=out_specs, check_vma=False)
```
